32 devices in a mesh: seq: 16 (over z, y, x), grp: 2 (over core).
Axes of the slice: x: 2, y: 2, z: 4, core: 2. Of those that a mesh axis runs over, the one named last changes fastest.
Arguments:
- inputs: bfloat16 [2048, 8192], P('seq', 'grp'), may hold values from -10 to 10
- query_states: bfloat16 [2048, 8192], P('seq', 'grp'), may hold values from -12 to 12
- key_states: bfloat16 [2048, 1024], P('seq', 'grp'), may hold values from -6 to 6
- value_states: bfloat16 [2048, 1024], P('seq', 'grp'), may hold values from -6 to 6
- doc_ids: int32 [2048], replicated, may hold values from 0 to 7, never falling along the last dimension, each value on 1 to 1536 neighbouring positions
- modality: int32 [2048], P('seq'), may hold values from 0 to 1, as said below
- expert_ids: int32 [2048, 4], P('seq'), may hold values from -1 to 15, as said below
- norm_gain: float32 [8192], P('grp'), may hold values from 0.1 to 1.9
- router_w: bfloat16 [8192, 32], P('grp'), may hold values from -0.0625 to 0.0625
- w_in: bfloat16 [2, 16, 8192, 1408], P(None, 'seq', 'grp'), may hold values from -1 to 1
- w_out: bfloat16 [2, 16, 1408, 8192], P(None, 'seq', None, 'grp'), may hold values from -2 to 2
- grad_out: bfloat16 [2048, 8192], P('seq', 'grp'), may hold values from -12 to 12
Outputs:
- layer_out: bfloat16 [2048, 8192], P('seq', 'grp')
- state_grad: bfloat16 [2048, 8192], P('seq', 'grp')
The draws below stay inside these ranges and needn't reach their ends.
Inputs may be any that keep to these rules, and one draw needn't show every extreme that they name: Modality is constant over aligned runs of 16 tokens; every block of 128 tokens held by one index of seq has a run of each modality. `expert_ids`: -1 marks an empty choice; the other entries of a token are distinct experts of its modality. At most 16 choices of the 128 tokens of one index of seq name one expert of one modality, and in every draw one text expert and one image expert are named by exactly 16 choices of every such block.
All inputs are finite; a program needn't handle non-finite values.
Results may differ from the reference program's by a relative error of at most 0.008.
Values may be sent and summed in bfloat16 or wider, within the bound.
No kernel may reach another device: no remote copies, remote signals or barrier semaphores. Data moves between devices by JAX's collectives and lax.ppermute only.
A program may use at most 128 MiB of HBM per device.

```python
import math
import jax
import jax.numpy as jnp
import numpy as np
from jax import lax

D = 8192
HEADS = 64
KV_HEADS = 8
HEAD_DIM = 128
FF = 1408
TOP = 4
DOCS = 8
LEN_DEV = 128
CAP = 16
EXPERTS = 16
TOKENS = 2048
N_SEQ = 16
N_GRP = 2


def route_plan(key):
    base_key = jax.random.fold_in(key, 17)
    k_kind, k_order, k_hot, k_score, k_empty = jax.random.split(base_key, 5)
    blocks = TOKENS // LEN_DEV
    run_count = LEN_DEV // CAP
    run_kinds = jax.random.randint(k_kind, (blocks, run_count), 0, 2)
    orders = jax.vmap(lambda one_key: jax.random.permutation(one_key, run_count))(jax.random.split(k_order, blocks))
    first_run = orders[:, 0]
    second = orders[:, 1]
    run_index = jnp.arange(run_count)[None, :]
    run_kinds = jnp.where(run_index == first_run[:, None], 0, run_kinds)
    run_kinds = jnp.where(run_index == second[:, None], 1, run_kinds)
    forced = (run_index == first_run[:, None]) | (run_index == second[:, None])
    modality = jnp.repeat(run_kinds, CAP, axis=1).reshape(TOKENS).astype(jnp.int32)
    forced_tok = jnp.repeat(forced, CAP, axis=1).reshape(TOKENS)
    hot_expert = jax.random.randint(k_hot, (2,), 0, EXPERTS)
    hot_tok = hot_expert[modality]
    expert_range = jnp.arange(EXPERTS, dtype=jnp.int32)[None, :]
    scores = jax.random.randint(k_score, (TOKENS, EXPERTS), 0, 1 << 20) * EXPERTS + expert_range
    boosted = scores + (forced_tok[:, None] & (expert_range == hot_tok[:, None])).astype(jnp.int32) * (1 << 28)
    choice_ids = lax.top_k(boosted, TOP)[1].astype(jnp.int32)
    empty_slot = (jax.random.randint(k_empty, (TOKENS, TOP), 0, 4) == 0) & (jnp.arange(TOP)[None, :] > 0)
    choice_ids = jnp.where(empty_slot, -1, choice_ids)
    column = modality[:, None] * EXPERTS + jnp.maximum(choice_ids, 0)
    one_hot = ((column[:, :, None] == jnp.arange(2 * EXPERTS)[None, None, :]) & (choice_ids[:, :, None] >= 0)).astype(jnp.int32)
    one_hot = one_hot.reshape(blocks, LEN_DEV * TOP, 2 * EXPERTS)
    earlier_count = jnp.cumsum(one_hot, axis=1) - one_hot
    slot_rank = jnp.sum(earlier_count * one_hot, axis=2).reshape(TOKENS, TOP)
    choice_ids = jnp.where(slot_rank >= CAP, -1, choice_ids)
    return (modality, choice_ids.astype(jnp.int32))


def draw_modality(key, part):
    return route_plan(key)[0]


def draw_expert_ids(key, part):
    return route_plan(key)[1]


def draw_query_states(key, part):
    own_key = jax.random.fold_in(key, 31)
    result = jnp.clip(jax.random.normal(own_key, (TOKENS, HEADS * HEAD_DIM)), -6.0, 6.0)
    return result.astype(jnp.float32).astype(jnp.bfloat16)


def draw_key_states(key, part):
    own_key = jax.random.fold_in(key, 37)
    result = jnp.clip(jax.random.normal(own_key, (TOKENS, KV_HEADS * HEAD_DIM)), -6.0, 6.0)
    return result.astype(jnp.float32).astype(jnp.bfloat16)


def feature_scale(key):
    order = jax.random.permutation(jax.random.fold_in(key, 47), 8)
    level = 0.25 * 10.0 ** (order.astype(jnp.float32) / 7.0)
    group = jnp.arange(D, dtype=jnp.int32) // (D // 8)
    return jnp.sqrt(level[group])


def drawn_stream(key):
    stream_key = jax.random.fold_in(key, 43)
    values = jnp.clip(jax.random.normal(stream_key, (TOKENS, D)), -6.0, 6.0)
    return values * feature_scale(key)[None, :]


def draw_inputs(key, part):
    result = drawn_stream(key)
    return result.astype(jnp.float32).astype(jnp.bfloat16)


def draw_grad_out(key, part):
    noise_key = jax.random.fold_in(key, 59)
    base_vals = drawn_stream(key)
    noise = jnp.clip(jax.random.normal(noise_key, (TOKENS, D)), -6.0, 6.0)
    return (0.9 * base_vals + 0.4 * noise).astype(jnp.float32).astype(jnp.bfloat16)


def unit_normal(sample_key, shape):
    return jnp.clip(jax.random.normal(sample_key, shape), -6.0, 6.0)


def expert_key(key, expert_index):
    return jax.random.fold_in(jax.random.fold_in(key, 53), expert_index)


def draw_w_in(key, part):
    sampler = unit_normal

    def one_expert(expert_index):
        base_vals = sampler(jax.random.fold_in(expert_key(key, expert_index), 1), (D, FF))
        return (base_vals * D ** (-0.5)).astype(jnp.float32).astype(jnp.bfloat16)
    stacked = lax.map(one_expert, jnp.arange(2 * EXPERTS, dtype=jnp.int32))
    return stacked.reshape(2, EXPERTS, D, FF)


def draw_w_out(key, part):
    sampler = unit_normal

    def one_expert(expert_index):
        own_key = expert_key(key, expert_index)
        base_vals = sampler(jax.random.fold_in(own_key, 1), (D, FF))
        noise = sampler(jax.random.fold_in(own_key, 2), (FF, D))
        mixed = (0.9 * base_vals.T + 0.4359 * noise) * FF ** (-0.5)
        return mixed.astype(jnp.float32).astype(jnp.bfloat16)
    stacked = lax.map(one_expert, jnp.arange(2 * EXPERTS, dtype=jnp.int32))
    return stacked.reshape(2, EXPERTS, FF, D)


def block_levels(key, dims, cuts, least, largest):
    gain, own = 1.0, jax.random.fold_in(key, 6)
    for dim, blocks in cuts:
        heights = jnp.exp(jax.random.uniform(jax.random.fold_in(own, dim), (blocks,), jnp.float32, least / len(cuts), largest / len(cuts)))
        gain = gain * jnp.repeat(heights, dims[dim] // blocks).reshape([-1 if axis == dim else 1 for axis in range(len(dims))])
    return gain


def split_up(amount, total, reach, lean):
    weights = [(1 << 20) // math.isqrt(standing ** lean) + 1 for standing in range(2, amount + 1)]
    rest, holding = total - reach - (amount - 1), [1] * (amount - 1)
    while rest > 0:
        candidates = [i for i in range(amount - 1) if holding[i] < reach]
        whole, left = sum([weights[i] for i in candidates]), rest
        for i in candidates:
            extra = min(reach - holding[i], max(1, left * weights[i] // whole), rest)
            holding[i] = holding[i] + extra
            rest = rest - extra
    return np.array([reach] + holding)


def ragged(key, number_of, total, limit, lean):
    if number_of == 2:
        one = jax.random.randint(key, (), max(1, total - limit), min(limit, total - 1) + 1)
        return jnp.stack([one, total - one])
    sizes = jnp.asarray(split_up(number_of, total, limit, lean), jnp.int32)
    pairs = (number_of - 1) // 2
    giver, receiver = sizes[1:1 + 2 * pairs:2], sizes[2:2 + 2 * pairs:2]
    margin = jnp.minimum(giver - 1, limit - receiver)
    moved = jax.random.randint(jax.random.fold_in(key, 1), (pairs,), 0, 1 << 20) % (margin + 1)
    sizes = sizes.at[1:1 + 2 * pairs:2].set(giver - moved).at[2:2 + 2 * pairs:2].set(receiver + moved)
    return sizes[jax.random.permutation(jax.random.fold_in(key, 2), number_of)]


def gaussian(rng, dims, deviation, reach, cuts=(), kind=jnp.bfloat16):
    entries = deviation * jax.random.normal(rng, dims, jnp.float32)
    if cuts:
        entries = entries * block_levels(rng, dims, cuts, -0.22, 0.18)
    return jnp.clip(entries, -reach, reach).astype(kind)


def setup_inputs(seed: int = 0) -> dict:
    seeds = jax.random.split(jax.random.key(seed), 13)
    inputs = draw_inputs(jax.random.fold_in(seeds[12], 71), 0)
    query_states = draw_query_states(jax.random.fold_in(seeds[12], 71), 0)
    key_states = draw_key_states(jax.random.fold_in(seeds[12], 71), 0)
    value_states = gaussian(seeds[3], (TOKENS, KV_HEADS * HEAD_DIM), 1.0, 6.0, ((0, 16), (1, 2)))
    doc_ids = jnp.searchsorted(jnp.cumsum(ragged(seeds[4], DOCS, TOKENS, 3 * TOKENS // 4, 2)), jnp.arange(TOKENS), side="right").astype(jnp.int32)
    modality = draw_modality(jax.random.fold_in(seeds[12], 71), 0)
    expert_ids = draw_expert_ids(jax.random.fold_in(seeds[12], 71), 0)
    norm_gain = jnp.clip(1.0 + 0.18 * jax.random.normal(seeds[7], (D,), jnp.float32), 0.1, 1.9)
    router_w = gaussian(seeds[8], (D, 2 * EXPERTS), D ** -0.5, 0.0625, ((0, 2),))
    w_in = draw_w_in(jax.random.fold_in(seeds[12], 71), 0)
    w_out = draw_w_out(jax.random.fold_in(seeds[12], 71), 0)
    grad_out = draw_grad_out(jax.random.fold_in(seeds[12], 71), 0)
    return dict(inputs=inputs, query_states=query_states, key_states=key_states, value_states=value_states, doc_ids=doc_ids, modality=modality, expert_ids=expert_ids, norm_gain=norm_gain, router_w=router_w, w_in=w_in, w_out=w_out, grad_out=grad_out)


eps_norm = 1e-05
gate_offset = 0.5

def gelu_back(pre_act, grad_in):
    return jax.vjp(lambda inner: jax.nn.gelu(inner, approximate=True), pre_act)[1](grad_in)[0]

def attention(query_states, key_states, value_states, doc_ids):
    group_size = HEADS // KV_HEADS
    query_heads = query_states.reshape(TOKENS, HEADS, HEAD_DIM).transpose(1, 0, 2)
    key_heads = key_states.reshape(TOKENS, KV_HEADS, HEAD_DIM).transpose(1, 0, 2)
    value_heads = value_states.reshape(TOKENS, KV_HEADS, HEAD_DIM).transpose(1, 0, 2)
    positions = jnp.arange(TOKENS, dtype=jnp.int32)
    allowed = (positions[None, :] <= positions[:, None]) & (doc_ids[None, :] == doc_ids[:, None])
    score_scale = HEAD_DIM ** (-0.5)

    def one_head(head_index):
        query_one = lax.dynamic_index_in_dim(query_heads, head_index, 0, keepdims=False)
        key_one = lax.dynamic_index_in_dim(key_heads, head_index // group_size, 0, keepdims=False)
        value_one = lax.dynamic_index_in_dim(value_heads, head_index // group_size, 0, keepdims=False)
        scores = jnp.dot(query_one, key_one.T, preferred_element_type=jnp.float32) * score_scale
        scores = jnp.where(allowed, scores, -1e+30)
        best_score = lax.optimization_barrier(jnp.max(scores, axis=1, keepdims=True))
        weights = jnp.where(allowed, jnp.exp(scores - best_score), 0.0)
        totals = lax.optimization_barrier(jnp.sum(weights, axis=1, keepdims=True))
        return jnp.dot(weights, value_one.astype(jnp.float32), precision=lax.Precision.HIGHEST) / totals
    head_out = lax.map(one_head, jnp.arange(HEADS, dtype=jnp.int32))
    return head_out.transpose(1, 0, 2).reshape(TOKENS, HEADS * HEAD_DIM).astype(jnp.bfloat16)

def expert_slots(modality, expert_ids):
    kept_mask = expert_ids >= 0
    column = modality[:, None] * EXPERTS + jnp.where(kept_mask, expert_ids, 0)
    one_hot = (column[:, :, None] == jnp.arange(2 * EXPERTS, dtype=jnp.int32)[None, None, :]) & kept_mask[:, :, None]
    counts = one_hot.astype(jnp.int32).reshape(N_SEQ, LEN_DEV * TOP, 2 * EXPERTS)
    earlier_count = jnp.cumsum(counts, axis=1) - counts
    slot_rank = lax.optimization_barrier(jnp.sum(earlier_count * counts, axis=2)).reshape(TOKENS, TOP)
    source = (jnp.arange(TOKENS, dtype=jnp.int32) // LEN_DEV)[:, None]
    slot_index = (column * N_SEQ + source) * CAP + slot_rank
    spare_row = 2 * EXPERTS * N_SEQ * CAP
    slot_index = jnp.where(kept_mask, slot_index, spare_row).astype(jnp.int32)
    return (kept_mask, one_hot, slot_index)

def fill_slots(entry_rows, slot_index):
    spare_row = 2 * EXPERTS * N_SEQ * CAP
    buffer = jnp.zeros((spare_row + 1, D), jnp.bfloat16)
    for choice_k in range(TOP):
        buffer = buffer.at[slot_index[:, choice_k]].set(entry_rows[choice_k])
    return buffer[:spare_row].reshape(2 * EXPERTS, N_SEQ * CAP, D)

def read_slots(buffer, slot_index):
    flat = jnp.concatenate([buffer.reshape(-1, D), jnp.zeros((1, D), jnp.bfloat16)], axis=0)
    return [flat[slot_index[:, choice_k]] for choice_k in range(TOP)]

def reference(inputs, query_states, key_states, value_states, doc_ids, modality, expert_ids, norm_gain, router_w, w_in, w_out, grad_out):
    attended = attention(query_states, key_states, value_states, doc_ids)
    resid_state = (inputs.astype(jnp.float32) + attended.astype(jnp.float32)).astype(jnp.bfloat16)
    state_wide = resid_state.astype(jnp.float32)
    inv_rms = lax.rsqrt(lax.optimization_barrier(jnp.mean(state_wide * state_wide, axis=1, keepdims=True)) + eps_norm)
    scaled = state_wide * norm_gain[None, :]
    normed = (scaled * inv_rms).astype(jnp.bfloat16)
    logits = jnp.dot(normed, router_w, preferred_element_type=jnp.float32)
    kept_mask, one_hot, slot_index = expert_slots(modality, expert_ids)
    kept_wide = kept_mask.astype(jnp.float32)
    chosen = lax.optimization_barrier(jnp.sum(jnp.where(one_hot, logits[:, None, :], 0.0), axis=2))
    lifted = jax.nn.sigmoid(chosen)
    denominator = gate_offset + lax.optimization_barrier(jnp.sum(kept_wide * lifted, axis=1, keepdims=True))
    gates = kept_wide * lifted / denominator
    slice_width = D // N_GRP
    w_in_all = w_in.reshape(2 * EXPERTS, D, FF)
    w_out_all = w_out.reshape(2 * EXPERTS, FF, D)
    sent_rows = fill_slots([normed] * TOP, slot_index)

    def forward_one(bundle):
        slot_rows, weight_in, weight_out = bundle
        partials = jnp.einsum('rgd,gdf->grf', slot_rows.reshape(-1, N_GRP, slice_width).astype(jnp.float32), weight_in.reshape(N_GRP, slice_width, FF).astype(jnp.float32))
        pre_act = lax.optimization_barrier(jnp.sum(lax.optimization_barrier(partials.astype(jnp.bfloat16)).astype(jnp.float32), axis=0))
        active = jax.nn.gelu(pre_act, approximate=True).astype(jnp.bfloat16)
        return (jnp.dot(active, weight_out, preferred_element_type=jnp.float32).astype(jnp.bfloat16), pre_act)
    expert_out, pre_all = lax.map(forward_one, (sent_rows, w_in_all, w_out_all))
    entry_out = read_slots(expert_out, slot_index)
    grad_wide = grad_out.astype(jnp.float32)
    mixture = jnp.zeros((TOKENS, D), jnp.float32)
    gate_cols = []
    for choice_k in range(TOP):
        out_wide = entry_out[choice_k].astype(jnp.float32)
        mixture = mixture + gates[:, choice_k:choice_k + 1] * out_wide
        gate_cols.append(lax.optimization_barrier(jnp.sum(grad_wide * out_wide, axis=1)))
    layer_out = (state_wide + mixture).astype(jnp.bfloat16)
    gate_grad = jnp.stack(gate_cols, axis=1)
    gate_dot = lax.optimization_barrier(jnp.sum(gates * gate_grad, axis=1, keepdims=True))
    logit_grad = kept_wide * (gate_grad - gate_dot) / denominator * lifted * (1.0 - lifted)
    logit_full = lax.optimization_barrier(jnp.sum(jnp.where(one_hot, logit_grad[:, :, None], 0.0), axis=1))
    router_grad = jnp.dot(logit_full, router_w.astype(jnp.float32).T, precision=lax.Precision.HIGHEST)
    grad_rows = [(gates[:, choice_k:choice_k + 1] * grad_wide).astype(jnp.bfloat16) for choice_k in range(TOP)]
    back_rows = fill_slots(grad_rows, slot_index)

    def backward_one(bundle):
        slot_rows, pre_act, weight_in, weight_out = bundle
        partials = jnp.einsum('rgd,fgd->grf', slot_rows.reshape(-1, N_GRP, slice_width).astype(jnp.float32), weight_out.reshape(FF, N_GRP, slice_width).astype(jnp.float32))
        act_grad = lax.optimization_barrier(jnp.sum(lax.optimization_barrier(partials.astype(jnp.bfloat16)).astype(jnp.float32), axis=0))
        pre_grad = gelu_back(pre_act, act_grad).astype(jnp.bfloat16)
        return jnp.dot(pre_grad, weight_in.T, preferred_element_type=jnp.float32).astype(jnp.bfloat16)
    entry_grad = lax.map(backward_one, (back_rows, pre_all, w_in_all, w_out_all))
    entry_back = read_slots(entry_grad, slot_index)
    normed_grad = router_grad
    for choice_k in range(TOP):
        normed_grad = normed_grad + entry_back[choice_k].astype(jnp.float32)
    norm_dot = lax.optimization_barrier(jnp.sum(normed_grad * scaled, axis=1, keepdims=True))
    state_grad = grad_wide + inv_rms * norm_gain[None, :] * normed_grad - inv_rms ** 3 / D * state_wide * norm_dot
    return (layer_out, state_grad.astype(jnp.bfloat16))
```

```python
import functools

import jax
import jax.numpy as jnp
from jax import lax
from jax.experimental import pallas as pl
from jax.experimental.pallas import tpu as pltpu
from jax.sharding import PartitionSpec as P


D = 8192
HEADS = 64
KV_HEADS = 8
HEAD_DIM = 128
TOP = 4
CAP = 16
CELL = 4
ROW_CHUNK = 256


eps_norm = 1e-05
gate_offset = 0.5
log2_scale = HEAD_DIM ** (-0.5) * 1.4426950408889634


def gelu_back(pre_act, grad_in):
    return jax.vjp(lambda inner: jax.nn.gelu(inner, approximate=True), pre_act)[1](grad_in)[0]


def row_total(partial_value):
    return lax.psum(partial_value, "grp")


def swap(block, distance):
    count = lax.axis_size("seq")
    return lax.ppermute(block, "seq", [(i, i ^ distance) for i in range(count)])


def half_exchange(buffers):
    half = lax.axis_size("seq") // 2
    groups = [list(range(half)), list(range(half, 2 * half))]
    return lax.all_to_all(
        buffers, "seq", split_axis=0, concat_axis=0, axis_index_groups=groups, tiled=True
    )


def far_swap(block):
    return swap(block, lax.axis_size("seq") // 2)


def whole_hidden(partial_value):
    rounded = partial_value.astype(jnp.bfloat16)
    members = lax.axis_size("grp")
    total = rounded.astype(jnp.float32)
    for step in range(1, members):
        pairs = [(i, (i + step) % members) for i in range(members)]
        total = total + lax.ppermute(rounded, "grp", pairs).astype(jnp.float32)
    return total


def gather_pieces(key_states, value_states, slot_index, grad_out):
    own = jnp.concatenate([key_states, value_states], axis=1)
    far_index = far_swap(slot_index)
    blocks = [own] + [swap(own, CELL * far) for far in range(1, lax.axis_size("seq") // CELL)]
    *_, grad_out, far_index = lax.optimization_barrier((*blocks[1:], grad_out, far_index))
    grad_far = far_swap(grad_out)
    pieces = []
    for far, block in enumerate(blocks):
        across = swap(block, 1)
        beside = swap(block, 2)
        corner = swap(beside, 1) if far % 2 == 0 else swap(across, 2)
        pieces.append((block, across, beside, corner))
    return pieces, far_index, grad_far


def attention_kernel(groups, group_heads, doc_s, me_s, q_ref, qdoc_ref, doc_ref, *refs):
    count = groups * CELL
    k_refs, v_refs = refs[:count], refs[count : 2 * count]
    out_ref, q_sc, k_sc, v_sc, bias_sc, m_sc, acc_sc = refs[2 * count :]
    length = q_ref.shape[0]
    span = CELL * length
    chunk = min(ROW_CHUNK, group_heads * length)
    me = me_s[0]
    for g in range(group_heads):
        q_sc[g * length : (g + 1) * length, :] = q_ref[:, g * HEAD_DIM : (g + 1) * HEAD_DIM]
    for i in range(count):
        k_sc[i * length : (i + 1) * length, :] = k_refs[i][...]
        v_sc[i * length : (i + 1) * length, :HEAD_DIM] = v_refs[i][...]
    v_sc[:, HEAD_DIM:] = jnp.ones_like(v_sc[:, HEAD_DIM:])
    m_sc[...] = jnp.full_like(m_sc, -1e30)
    acc_sc[...] = jnp.zeros_like(acc_sc)
    first_doc = doc_s[me * length]
    row_pos = lax.broadcasted_iota(jnp.int32, (length, length), 0)
    col_pos = lax.broadcasted_iota(jnp.int32, (length, length), 1)

    def group(far, carry):
        wanted = jnp.int32(0)
        for c in range(CELL):
            block = jnp.bitwise_xor(me, far * CELL + c)
            near = (block <= me) & (doc_s[block * length + length - 1] >= first_doc)
            wanted = wanted + near.astype(jnp.int32)

        @pl.when(wanted > 0)
        def _():
            for c in range(CELL):
                block = jnp.bitwise_xor(me, far * CELL + c)
                allowed = (block * length + col_pos <= me * length + row_pos) & (
                    doc_ref[pl.ds(block, 1), :] == qdoc_ref[...]
                )
                bias = jnp.where(allowed, 0.0, -1e30)
                for r in range(chunk // length):
                    bias_sc[r * length : (r + 1) * length, c * length : (c + 1) * length] = bias
            start = pl.multiple_of(far * span, span)
            keys = k_sc[pl.ds(start, span), :]
            values = v_sc[pl.ds(start, span), :]
            for r in range(group_heads * length // chunk):
                rows = slice(r * chunk, (r + 1) * chunk)
                scores = (
                    lax.dot_general(
                        q_sc[rows, :],
                        keys,
                        (((1,), (1,)), ((), ())),
                        preferred_element_type=jnp.float32,
                    )
                    + bias_sc[...]
                )
                old = m_sc[rows, :]
                new = jnp.maximum(old, jnp.max(scores, axis=1, keepdims=True))
                weights = jnp.exp2((scores - new) * log2_scale)
                fade = jnp.exp2((old - new) * log2_scale)
                acc_sc[rows, :] = acc_sc[rows, :] * fade + jnp.dot(
                    weights.astype(jnp.bfloat16), values, preferred_element_type=jnp.float32
                )
                m_sc[rows, :] = new

        return carry

    lax.fori_loop(0, groups, group, 0)
    for g in range(group_heads):
        rows = slice(g * length, (g + 1) * length)
        out_ref[:, g * HEAD_DIM : (g + 1) * HEAD_DIM] = (
            acc_sc[rows, :HEAD_DIM] / acc_sc[rows, HEAD_DIM:]
        ).astype(out_ref.dtype)


def attend(query_states, pieces, doc_ids):
    length, width_local = query_states.shape
    groups = len(pieces)
    count = groups * CELL
    kv_local = pieces[0][0].shape[1] // (2 * HEAD_DIM)
    group_heads = HEADS // KV_HEADS
    flat = [piece for group in pieces for piece in group]
    me = lax.axis_index("seq").astype(jnp.int32)
    query_doc = lax.dynamic_slice_in_dim(doc_ids, me * length, length).reshape(length, 1)
    rows = group_heads * length
    chunk = min(ROW_CHUNK, rows)
    query_spec = pl.BlockSpec((length, group_heads * HEAD_DIM), lambda h, *_: (0, h))
    key_spec = pl.BlockSpec((length, HEAD_DIM), lambda h, *_: (0, h))
    value_spec = pl.BlockSpec((length, HEAD_DIM), lambda h, *_: (0, kv_local + h))
    return pl.pallas_call(
        functools.partial(attention_kernel, groups, group_heads),
        out_shape=jax.ShapeDtypeStruct((length, width_local), jnp.bfloat16),
        grid_spec=pltpu.PrefetchScalarGridSpec(
            num_scalar_prefetch=2,
            grid=(kv_local,),
            in_specs=[
                query_spec,
                pl.BlockSpec((length, 1), lambda h, *_: (0, 0)),
                pl.BlockSpec((count, length), lambda h, *_: (0, 0)),
            ]
            + [key_spec] * count
            + [value_spec] * count,
            out_specs=query_spec,
            scratch_shapes=[
                pltpu.VMEM((rows, HEAD_DIM), jnp.bfloat16),
                pltpu.VMEM((count * length, HEAD_DIM), jnp.bfloat16),
                pltpu.VMEM((count * length, 2 * HEAD_DIM), jnp.bfloat16),
                pltpu.VMEM((chunk, CELL * length), jnp.float32),
                pltpu.VMEM((rows, 1), jnp.float32),
                pltpu.VMEM((rows, 2 * HEAD_DIM), jnp.float32),
            ],
        ),
        compiler_params=pltpu.CompilerParams(vmem_limit_bytes=60 << 20),
        cost_estimate=pl.CostEstimate(
            flops=6 * kv_local * rows * count * length * HEAD_DIM,
            bytes_accessed=4 * length * width_local + 4 * count * length * kv_local * HEAD_DIM,
            transcendentals=kv_local * rows * count * length,
        ),
        name="attend",
    )(doc_ids, me[None], query_states, query_doc, doc_ids.reshape(count, length), *flat, *flat)


def split_three(exact):
    high = exact.astype(jnp.bfloat16)
    rest = exact - high.astype(jnp.float32)
    middle = rest.astype(jnp.bfloat16)
    low = (rest - middle.astype(jnp.float32)).astype(jnp.bfloat16)
    return high, middle, low


def packed_tail(columns):
    rows = columns[0].shape[0]
    lane = lax.broadcasted_iota(jnp.int32, (rows, HEAD_DIM), 1)
    spread = jnp.zeros((rows, HEAD_DIM), jnp.float32)
    for part in range(3):
        for k, column in enumerate(columns):
            spread = jnp.where(lane == part * TOP + k, column, spread)
    high, middle, low = [part.astype(jnp.float32) for part in split_three(spread)]
    chosen = jnp.where(lane < TOP, high, jnp.where(lane < 2 * TOP, middle, low))
    return chosen.astype(jnp.bfloat16)


def unpack_tail(tail, amount):
    parts = [tail[:, part * TOP : part * TOP + amount].astype(jnp.float32) for part in range(3)]
    return parts[0] + parts[1] + parts[2]


def block_width(width):
    return min(512, width)


def pick_kernel(normalize, near_codes, far_codes, near_place, far_place, *refs):
    if normalize:
        gain, near_inv, far_inv, near_x, far_x, first_out, second_out, hot, stacked = refs
    else:
        near_x, far_x, first_out, second_out, hot, stacked = refs
    length = near_x.shape[0]

    @pl.when(pl.program_id(0) == 0)
    def _():
        for side, (codes, place) in enumerate(((near_codes, near_place), (far_codes, far_place))):
            total = jnp.zeros((hot.shape[0], length), jnp.float32)
            for k in range(TOP):
                total = total + jnp.where(place[...] == codes[k : k + 1, :], 1.0, 0.0)
            hot[:, side * length : (side + 1) * length] = total.astype(jnp.bfloat16)

    near_rows, far_rows = near_x[...], far_x[...]
    if normalize:
        near_rows, far_rows = [
            ((rows.astype(jnp.float32) * gain[...]) * inv[...]).astype(jnp.bfloat16)
            for rows, inv in ((near_rows, near_inv), (far_rows, far_inv))
        ]
    stacked[:length, :] = near_rows
    stacked[length:, :] = far_rows
    slots = first_out.shape[0]
    for part, out in enumerate((first_out, second_out)):
        out[...] = jnp.dot(
            hot[part * slots : (part + 1) * slots, :],
            stacked[...],
            preferred_element_type=jnp.float32,
        ).astype(jnp.bfloat16)


def fixed(shape):
    return pl.BlockSpec(shape, lambda i: (0,) * len(shape))


def pick(code_rows, place_columns, rows_pair, norm=None):
    length, width = rows_pair[0].shape
    all_slots = place_columns[0].shape[0]
    slots = all_slots // 2
    step = block_width(width)
    block = pl.BlockSpec((length, step), lambda i: (0, i))
    extra, extra_specs = (), []
    if norm is not None:
        gain, near_inv, far_inv = norm
        extra = (gain, near_inv, far_inv)
        extra_specs = [pl.BlockSpec((1, step), lambda i: (0, i))] + [fixed((length, 1))] * 2
    return pl.pallas_call(
        functools.partial(pick_kernel, norm is not None),
        out_shape=[jax.ShapeDtypeStruct((slots, width), jnp.bfloat16)] * 2,
        grid=(width // step,),
        in_specs=[fixed((TOP, length))] * 2
        + [fixed((all_slots, 1))] * 2
        + extra_specs
        + [block] * 2,
        out_specs=[pl.BlockSpec((slots, step), lambda i: (0, i))] * 2,
        scratch_shapes=[
            pltpu.VMEM((all_slots, 2 * length), jnp.bfloat16),
            pltpu.VMEM((2 * length, step), jnp.bfloat16),
        ],
        compiler_params=pltpu.CompilerParams(vmem_limit_bytes=24 << 20),
        cost_estimate=pl.CostEstimate(
            flops=4 * all_slots * length * width,
            bytes_accessed=2 * width * (2 * length + all_slots),
            transcendentals=0,
        ),
        name="pick_normed" if norm is not None else "pick",
    )(*code_rows, *place_columns, *extra, *rows_pair)


def gate_matrix(codes, place, gates, high, low):
    length = codes[0].shape[0]
    for side in (0, 1):
        exact = jnp.zeros((length, high.shape[1]), jnp.float32)
        for k in range(TOP):
            exact = jnp.where(
                codes[side][:, k : k + 1] == place[side][...], gates[side][:, k : k + 1], exact
            )
        rows = slice(side * length, (side + 1) * length)
        high_part = exact.astype(jnp.bfloat16)
        high[rows, :] = high_part
        low[rows, :] = (exact - high_part.astype(jnp.float32)).astype(jnp.bfloat16)


def weighted(high, low, first, second):
    slots = first.shape[0]
    total = None
    for matrix in (high, low):
        for columns, rows in ((slice(0, slots), first), (slice(slots, 2 * slots), second)):
            term = jnp.dot(matrix[:, columns], rows[...], preferred_element_type=jnp.float32)
            total = term if total is None else total + term
    return total


def forward_kernel(*refs):
    codes, place, gates = refs[0:2], refs[2:4], refs[4:6]
    first, second, near_g, far_g, state, near_out, far_out, sums_out, high, low, overlap = refs[6:]
    length, step = near_out.shape
    slots = first.shape[0]
    index = pl.program_id(0)

    @pl.when(index == 0)
    def _():
        gate_matrix(codes, place, gates, high, low)
        overlap[...] = jnp.zeros_like(overlap)

    mixed = weighted(high, low, first, second)
    near_out[...] = mixed[:length] + state[...].astype(jnp.float32)
    far_out[:, pl.ds(pl.multiple_of(index * step, step), step)] = mixed[length:].astype(
        jnp.bfloat16
    )
    for side, grads in enumerate((near_g, far_g)):
        for part, rows in enumerate((first, second)):
            overlap[
                side * length : (side + 1) * length, part * slots : (part + 1) * slots
            ] += lax.dot_general(
                grads[...], rows[...], (((1,), (1,)), ((), ())), preferred_element_type=jnp.float32
            )

    @pl.when(index == pl.num_programs(0) - 1)
    def _():
        sums = [
            [
                jnp.sum(
                    jnp.where(
                        codes[side][:, k : k + 1] == place[side][...],
                        overlap[side * length : (side + 1) * length, :],
                        0.0,
                    ),
                    axis=1,
                    keepdims=True,
                )
                for k in range(TOP)
            ]
            for side in (0, 1)
        ]
        lane = lax.broadcasted_iota(jnp.int32, sums_out.shape, 1)
        spread = jnp.zeros(sums_out.shape, jnp.float32)
        for k in range(TOP):
            spread = jnp.where(lane == k, sums[0][k], spread)
        sums_out[...] = spread
        far_out[:, far_out.shape[1] - HEAD_DIM :] = packed_tail(sums[1])


def combine_forward(codes, place, gates, first, second, grad_pair, state):
    length, width = state.shape
    slots = first.shape[0]
    step = block_width(width)
    block = pl.BlockSpec((length, step), lambda i: (0, i))
    slot_block = pl.BlockSpec((slots, step), lambda i: (0, i))
    return pl.pallas_call(
        forward_kernel,
        out_shape=[
            jax.ShapeDtypeStruct((length, width), jnp.float32),
            jax.ShapeDtypeStruct((length, width + HEAD_DIM), jnp.bfloat16),
            jax.ShapeDtypeStruct((length, HEAD_DIM), jnp.float32),
        ],
        grid=(width // step,),
        in_specs=[fixed((length, TOP))] * 2
        + [fixed((1, 2 * slots))] * 2
        + [fixed((length, TOP))] * 2
        + [slot_block] * 2
        + [block] * 3,
        out_specs=[block, fixed((length, width + HEAD_DIM)), fixed((length, HEAD_DIM))],
        scratch_shapes=[pltpu.VMEM((2 * length, 2 * slots), jnp.bfloat16)] * 2
        + [pltpu.VMEM((2 * length, 2 * slots), jnp.float32)],
        compiler_params=pltpu.CompilerParams(vmem_limit_bytes=24 << 20),
        cost_estimate=pl.CostEstimate(
            flops=24 * length * slots * width,
            bytes_accessed=4 * slots * width + 12 * length * width,
            transcendentals=0,
        ),
        name="combine_forward",
    )(*codes, *place, *gates, first, second, *grad_pair, state)


def backward_kernel(*refs):
    codes, place, gates = refs[0:2], refs[2:4], refs[4:6]
    first, second, near_state, far_state, gain = refs[6:11]
    near_out, early_out, late_out, dot_out, high, low, near_dot, far_dot = refs[11:]
    length, step = near_out.shape
    index = pl.program_id(0)
    half_steps = pl.num_programs(0) // 2

    @pl.when(index == 0)
    def _():
        gate_matrix(codes, place, gates, high, low)
        near_dot[...] = jnp.zeros_like(near_dot)
        far_dot[...] = jnp.zeros_like(far_dot)

    mixed = weighted(high, low, first, second)
    near = mixed[:length]
    far = mixed[length:]
    near_out[...] = near
    near_dot[...] += jnp.sum(
        near * (near_state[...].astype(jnp.float32) * gain[...]), axis=1, keepdims=True
    )
    far_dot[...] += jnp.sum(
        far * (far_state[...].astype(jnp.float32) * gain[...]), axis=1, keepdims=True
    )

    @pl.when(index < half_steps)
    def _():
        early_out[:, pl.ds(pl.multiple_of(index * step, step), step)] = far.astype(jnp.bfloat16)

    @pl.when(index >= half_steps)
    def _():
        start = pl.multiple_of((index - half_steps) * step, step)
        late_out[:, pl.ds(start, step)] = far.astype(jnp.bfloat16)

    @pl.when(index == pl.num_programs(0) - 1)
    def _():
        early_out[:, early_out.shape[1] - HEAD_DIM :] = packed_tail([far_dot[...]])
        dot_out[...] = near_dot[...]


def combine_backward(codes, place, gates, first, second, state_pair, gain):
    length, width = state_pair[0].shape
    slots = first.shape[0]
    step = min(block_width(width), width // 2)
    block = pl.BlockSpec((length, step), lambda i: (0, i))
    slot_block = pl.BlockSpec((slots, step), lambda i: (0, i))
    return pl.pallas_call(
        backward_kernel,
        out_shape=[
            jax.ShapeDtypeStruct((length, width), jnp.float32),
            jax.ShapeDtypeStruct((length, width // 2 + HEAD_DIM), jnp.bfloat16),
            jax.ShapeDtypeStruct((length, width // 2), jnp.bfloat16),
            jax.ShapeDtypeStruct((length, 1), jnp.float32),
        ],
        grid=(width // step,),
        in_specs=[fixed((length, TOP))] * 2
        + [fixed((1, 2 * slots))] * 2
        + [fixed((length, TOP))] * 2
        + [slot_block] * 2
        + [block] * 2
        + [pl.BlockSpec((1, step), lambda i: (0, i))],
        out_specs=[
            block,
            fixed((length, width // 2 + HEAD_DIM)),
            fixed((length, width // 2)),
            fixed((length, 1)),
        ],
        scratch_shapes=[pltpu.VMEM((2 * length, 2 * slots), jnp.bfloat16)] * 2
        + [pltpu.VMEM((length, 1), jnp.float32)] * 2,
        compiler_params=pltpu.CompilerParams(vmem_limit_bytes=24 << 20),
        cost_estimate=pl.CostEstimate(
            flops=16 * length * slots * width,
            bytes_accessed=4 * slots * width + 14 * length * width,
            transcendentals=0,
        ),
        name="combine_backward",
    )(*codes, *place, *gates, first, second, *state_pair, gain)


def body(
    inputs,
    query_states,
    key_states,
    value_states,
    doc_ids,
    modality,
    expert_ids,
    norm_gain,
    router_w,
    w_in,
    w_out,
    grad_out,
):
    length, width_local = inputs.shape
    experts = lax.axis_size("seq")
    half = experts // 2
    slots = experts * CAP
    kinds = (0, 1)

    kept_mask = expert_ids >= 0
    kept_wide = kept_mask.astype(jnp.float32)
    column = modality[:, None] * experts + jnp.where(kept_mask, expert_ids, 0)
    one_hot = (
        column[:, :, None] == jnp.arange(2 * experts, dtype=jnp.int32)[None, None, :]
    ) & kept_mask[:, :, None]
    entries = length * TOP
    flat_hot = one_hot.reshape(entries, 2 * experts).astype(jnp.bfloat16)
    entry_range = jnp.arange(entries, dtype=jnp.int32)
    earlier = (entry_range[:, None] > entry_range[None, :]).astype(jnp.bfloat16)
    before = jnp.dot(earlier, flat_hot, preferred_element_type=jnp.float32)
    slot_rank = jnp.sum(before * flat_hot.astype(jnp.float32), axis=1).astype(jnp.int32)
    slot_index = jnp.where(kept_mask, column * CAP + slot_rank.reshape(length, TOP), -1)

    position = jnp.arange(2 * slots, dtype=jnp.int32)
    local = position % slots
    first = lax.axis_index("seq") // half * half * CAP
    place = position // slots * slots + first + local // (2 * CAP) * CAP + local % CAP
    side_of = local // CAP % 2
    places = [jnp.where(side_of == side, place, -2) for side in (0, 1)]
    place_rows = [one.reshape(1, 2 * slots) for one in places]
    place_columns = [one.reshape(2 * slots, 1) for one in places]

    pieces, far_index, grad_far = gather_pieces(key_states, value_states, slot_index, grad_out)
    codes = [slot_index, far_index]
    code_rows = [one.T for one in codes]
    grad_pair = [grad_out, grad_far]

    def send(picked):
        return half_exchange(picked.reshape(half, 2 * CAP, width_local)).reshape(slots, width_local)

    def give_back(rows):
        return send(rows.astype(jnp.bfloat16))

    attended = attend(query_states, pieces, doc_ids)
    resid_state = (inputs.astype(jnp.float32) + attended.astype(jnp.float32)).astype(jnp.bfloat16)
    _, *grad_pair = lax.optimization_barrier((resid_state, *grad_pair))
    got_grads = [send(picked) for picked in pick(code_rows, place_columns, grad_pair)]
    state_pair = [resid_state, far_swap(resid_state)]
    state_wide = resid_state.astype(jnp.float32)
    gain = norm_gain[None, :]
    squares = row_total(jnp.sum(state_wide * state_wide, axis=1))
    inv_rms = lax.rsqrt(squares / D + eps_norm)[:, None]
    normed = (state_wide * gain * inv_rms).astype(jnp.bfloat16)
    logits = row_total(jnp.dot(normed, router_w, preferred_element_type=jnp.float32))
    chosen = jnp.sum(jnp.where(one_hot, logits[:, None, :], 0.0), axis=2)
    lifted = jax.nn.sigmoid(chosen)
    denominator = gate_offset + jnp.sum(kept_wide * lifted, axis=1, keepdims=True)
    gates = kept_wide * lifted / denominator
    far_scalars = far_swap(jnp.concatenate([gates, inv_rms], axis=1))
    gate_pair = [gates, far_scalars[:, :TOP]]
    far_inv = far_scalars[:, TOP:]

    got_rows = [
        send(picked)
        for picked in pick(code_rows, place_columns, state_pair, (gain, inv_rms, far_inv))
    ]

    act_grads = [
        whole_hidden(
            lax.dot_general(
                got_grads[kind],
                w_out[kind, 0],
                (((1,), (1,)), ((), ())),
                preferred_element_type=jnp.float32,
            )
        )
        for kind in kinds
    ]
    returned = []
    entry_grads = []
    for kind in kinds:
        pre_act = whole_hidden(
            jnp.dot(got_rows[kind], w_in[kind, 0], preferred_element_type=jnp.float32)
        )
        active = jax.nn.gelu(pre_act, approximate=True).astype(jnp.bfloat16)
        returned.append(
            give_back(jnp.dot(active, w_out[kind, 0], preferred_element_type=jnp.float32))
        )
        pre_grad = gelu_back(pre_act, act_grads[kind]).astype(jnp.bfloat16)
        entry_grads.append(
            lax.dot_general(
                pre_grad,
                w_in[kind, 0],
                (((1,), (1,)), ((), ())),
                preferred_element_type=jnp.float32,
            )
        )
    near_sum, far_sum, near_overlap = combine_forward(
        codes, place_rows, gate_pair, *returned, grad_pair, resid_state
    )
    got_sum = far_swap(far_sum)
    layer_out = (near_sum + got_sum[:, :width_local].astype(jnp.float32)).astype(jnp.bfloat16)

    gate_grad = row_total(near_overlap[:, :TOP] + unpack_tail(got_sum[:, width_local:], TOP))
    gate_dot = jnp.sum(gates * gate_grad, axis=1, keepdims=True)
    logit_grad = kept_wide * (gate_grad - gate_dot) / denominator * lifted * (1.0 - lifted)
    logit_full = jnp.sum(jnp.where(one_hot, logit_grad[:, :, None], 0.0), axis=1)
    router_grad = jnp.dot(
        logit_full, router_w.astype(jnp.float32).T, precision=lax.Precision.HIGHEST
    )
    grads_back = [give_back(entry_grads[kind]) for kind in kinds]
    near_grad, far_early, far_late, near_dot = combine_backward(
        codes, place_rows, gate_pair, *grads_back, state_pair, gain
    )
    got_early = far_swap(far_early)
    got_late = far_swap(far_late)
    cut = width_local // 2
    router_dot = jnp.sum(router_grad * (state_wide * gain), axis=1, keepdims=True)
    norm_dot = row_total(near_dot + router_dot + unpack_tail(got_early[:, cut:], 1))
    got_grad = jnp.concatenate([got_early[:, :cut], got_late], axis=1)
    state_grad = (
        grad_out.astype(jnp.float32)
        + inv_rms * gain * (router_grad + near_grad + got_grad.astype(jnp.float32))
        - inv_rms**3 / D * state_wide * norm_dot
    )
    return (layer_out, state_grad.astype(jnp.bfloat16))


def solution(mesh):
    in_specs = (
        P("seq", "grp"),
        P("seq", "grp"),
        P("seq", "grp"),
        P("seq", "grp"),
        P(),
        P("seq"),
        P("seq", None),
        P("grp"),
        P("grp", None),
        P(None, "seq", "grp", None),
        P(None, "seq", None, "grp"),
        P("seq", "grp"),
    )
    out_specs = (P("seq", "grp"), P("seq", "grp"))

    return jax.shard_map(body, mesh=mesh, in_specs=in_specs, out_specs=out_specs, check_vma=False)
```

```python
import functools

import jax
import jax.numpy as jnp
from jax import lax
from jax.experimental import pallas as pl
from jax.experimental.pallas import tpu as pltpu
from jax.sharding import PartitionSpec as P


D = 8192
HEADS = 64
KV_HEADS = 8
HEAD_DIM = 128
TOP = 4
CAP = 16
CELL = 4
ROW_CHUNK = 256


eps_norm = 1e-05
gate_offset = 0.5
log2_scale = HEAD_DIM ** (-0.5) * 1.4426950408889634


def gelu_back(pre_act, grad_in):
    return jax.vjp(lambda inner: jax.nn.gelu(inner, approximate=True), pre_act)[1](grad_in)[0]


def row_total(partial_value):
    return lax.psum(partial_value, "grp")


def swap(block, distance):
    count = lax.axis_size("seq")
    return lax.ppermute(block, "seq", [(i, i ^ distance) for i in range(count)])


def half_exchange(buffers):
    half = lax.axis_size("seq") // 2
    groups = [list(range(half)), list(range(half, 2 * half))]
    return lax.all_to_all(
        buffers, "seq", split_axis=0, concat_axis=0, axis_index_groups=groups, tiled=True
    )


def far_swap(block):
    return swap(block, lax.axis_size("seq") // 2)


def whole_hidden(rounded):
    members = lax.axis_size("grp")
    total = rounded.astype(jnp.float32)
    for step in range(1, members):
        pairs = [(i, (i + step) % members) for i in range(members)]
        total = total + lax.ppermute(rounded, "grp", pairs).astype(jnp.float32)
    return total


def gather_pieces(key_states, value_states, slot_index, grad_out):
    own = jnp.concatenate([key_states, value_states], axis=1)
    blocks = [own] + [swap(own, CELL * far) for far in range(1, lax.axis_size("seq") // CELL)]
    far_index = far_swap(slot_index)
    grad_far = far_swap(grad_out[:, : grad_out.shape[1] // 2])
    pieces = []
    for far, block in enumerate(blocks):
        across = swap(block, 1)
        beside = swap(block, 2)
        corner = swap(beside, 1) if far % 2 == 0 else swap(across, 2)
        pieces.append((block, across, beside, corner))
    return pieces, far_index, grad_far


def attention_kernel(groups, group_heads, doc_s, me_s, q_ref, qdoc_ref, doc_ref, *refs):
    count = groups * CELL
    k_refs, v_refs = refs[:count], refs[count : 2 * count]
    out_ref, q_sc, k_sc, v_sc, bias_sc, m_sc, acc_sc = refs[2 * count :]
    length = q_ref.shape[0]
    span = CELL * length
    chunk = min(ROW_CHUNK, group_heads * length)
    me = me_s[0]
    for g in range(group_heads):
        q_sc[g * length : (g + 1) * length, :] = q_ref[:, g * HEAD_DIM : (g + 1) * HEAD_DIM]
    for i in range(count):
        k_sc[i * length : (i + 1) * length, :] = k_refs[i][...]
        v_sc[i * length : (i + 1) * length, :HEAD_DIM] = v_refs[i][...]
    v_sc[:, HEAD_DIM:] = jnp.ones_like(v_sc[:, HEAD_DIM:])
    m_sc[...] = jnp.full_like(m_sc, -1e30)
    acc_sc[...] = jnp.zeros_like(acc_sc)
    first_doc = doc_s[me * length]
    row_pos = lax.broadcasted_iota(jnp.int32, (length, length), 0)
    col_pos = lax.broadcasted_iota(jnp.int32, (length, length), 1)

    def group(far, carry):
        wanted = jnp.int32(0)
        for c in range(CELL):
            block = jnp.bitwise_xor(me, far * CELL + c)
            near = (block <= me) & (doc_s[block * length + length - 1] >= first_doc)
            wanted = wanted + near.astype(jnp.int32)

        @pl.when(wanted > 0)
        def _():
            for c in range(CELL):
                block = jnp.bitwise_xor(me, far * CELL + c)
                allowed = (block * length + col_pos <= me * length + row_pos) & (
                    doc_ref[pl.ds(block, 1), :] == qdoc_ref[...]
                )
                bias = jnp.where(allowed, 0.0, -1e30)
                for r in range(chunk // length):
                    bias_sc[r * length : (r + 1) * length, c * length : (c + 1) * length] = bias
            start = pl.multiple_of(far * span, span)
            keys = k_sc[pl.ds(start, span), :]
            values = v_sc[pl.ds(start, span), :]
            for r in range(group_heads * length // chunk):
                rows = slice(r * chunk, (r + 1) * chunk)
                scores = (
                    lax.dot_general(
                        q_sc[rows, :],
                        keys,
                        (((1,), (1,)), ((), ())),
                        preferred_element_type=jnp.float32,
                    )
                    + bias_sc[...]
                )
                old = m_sc[rows, :]
                new = jnp.maximum(old, jnp.max(scores, axis=1, keepdims=True))
                weights = jnp.exp2((scores - new) * log2_scale)
                fade = jnp.exp2((old - new) * log2_scale)
                acc_sc[rows, :] = acc_sc[rows, :] * fade + jnp.dot(
                    weights.astype(jnp.bfloat16), values, preferred_element_type=jnp.float32
                )
                m_sc[rows, :] = new

        return carry

    lax.fori_loop(0, groups, group, 0)
    for g in range(group_heads):
        rows = slice(g * length, (g + 1) * length)
        out_ref[:, g * HEAD_DIM : (g + 1) * HEAD_DIM] = (
            acc_sc[rows, :HEAD_DIM] / acc_sc[rows, HEAD_DIM:]
        ).astype(out_ref.dtype)


def attend(query_states, pieces, doc_ids):
    length, width_local = query_states.shape
    groups = len(pieces)
    count = groups * CELL
    kv_local = pieces[0][0].shape[1] // (2 * HEAD_DIM)
    group_heads = HEADS // KV_HEADS
    flat = [piece for group in pieces for piece in group]
    me = lax.axis_index("seq").astype(jnp.int32)
    query_doc = lax.dynamic_slice_in_dim(doc_ids, me * length, length).reshape(length, 1)
    rows = group_heads * length
    chunk = min(ROW_CHUNK, rows)
    query_spec = pl.BlockSpec((length, group_heads * HEAD_DIM), lambda h, *_: (0, h))
    key_spec = pl.BlockSpec((length, HEAD_DIM), lambda h, *_: (0, h))
    value_spec = pl.BlockSpec((length, HEAD_DIM), lambda h, *_: (0, kv_local + h))
    return pl.pallas_call(
        functools.partial(attention_kernel, groups, group_heads),
        out_shape=jax.ShapeDtypeStruct((length, width_local), jnp.bfloat16),
        grid_spec=pltpu.PrefetchScalarGridSpec(
            num_scalar_prefetch=2,
            grid=(kv_local,),
            in_specs=[
                query_spec,
                pl.BlockSpec((length, 1), lambda h, *_: (0, 0)),
                pl.BlockSpec((count, length), lambda h, *_: (0, 0)),
            ]
            + [key_spec] * count
            + [value_spec] * count,
            out_specs=query_spec,
            scratch_shapes=[
                pltpu.VMEM((rows, HEAD_DIM), jnp.bfloat16),
                pltpu.VMEM((count * length, HEAD_DIM), jnp.bfloat16),
                pltpu.VMEM((count * length, 2 * HEAD_DIM), jnp.bfloat16),
                pltpu.VMEM((chunk, CELL * length), jnp.float32),
                pltpu.VMEM((rows, 1), jnp.float32),
                pltpu.VMEM((rows, 2 * HEAD_DIM), jnp.float32),
            ],
        ),
        compiler_params=pltpu.CompilerParams(vmem_limit_bytes=60 << 20),
        cost_estimate=pl.CostEstimate(
            flops=6 * kv_local * rows * count * length * HEAD_DIM,
            bytes_accessed=4 * length * width_local + 4 * count * length * kv_local * HEAD_DIM,
            transcendentals=kv_local * rows * count * length,
        ),
        name="attend",
    )(doc_ids, me[None], query_states, query_doc, doc_ids.reshape(count, length), *flat, *flat)


def split_three(exact):
    high = exact.astype(jnp.bfloat16)
    rest = exact - high.astype(jnp.float32)
    middle = rest.astype(jnp.bfloat16)
    low = (rest - middle.astype(jnp.float32)).astype(jnp.bfloat16)
    return high, middle, low


def packed_tail(columns):
    rows = columns[0].shape[0]
    lane = lax.broadcasted_iota(jnp.int32, (rows, HEAD_DIM), 1)
    spread = jnp.zeros((rows, HEAD_DIM), jnp.float32)
    for part in range(3):
        for k, column in enumerate(columns):
            spread = jnp.where(lane == part * TOP + k, column, spread)
    high, middle, low = [part.astype(jnp.float32) for part in split_three(spread)]
    chosen = jnp.where(lane < TOP, high, jnp.where(lane < 2 * TOP, middle, low))
    return chosen.astype(jnp.bfloat16)


def unpack_tail(tail, amount):
    parts = [tail[:, part * TOP : part * TOP + amount].astype(jnp.float32) for part in range(3)]
    return parts[0] + parts[1] + parts[2]


def block_width(width):
    return min(512, width)


def pick_kernel(normalize, near_codes, far_codes, near_place, far_place, *refs):
    if normalize:
        gain, near_inv, far_inv, near_x, far_x, *outs, hot, stacked = refs
    else:
        near_x, far_x, *outs, hot, stacked = refs
    length = near_x.shape[0]

    @pl.when(pl.program_id(0) == 0)
    def _():
        for side, (codes, place) in enumerate(((near_codes, near_place), (far_codes, far_place))):
            total = jnp.zeros((hot.shape[0], length), jnp.float32)
            for k in range(TOP):
                total = total + jnp.where(place[...] == codes[k : k + 1, :], 1.0, 0.0)
            hot[:, side * length : (side + 1) * length] = total.astype(jnp.bfloat16)

    near_rows, far_rows = near_x[...], far_x[...]
    if normalize:
        near_rows, far_rows = [
            ((rows.astype(jnp.float32) * gain[...]) * inv[...]).astype(jnp.bfloat16)
            for rows, inv in ((near_rows, near_inv), (far_rows, far_inv))
        ]
    stacked[:length, :] = near_rows
    stacked[length:, :] = far_rows
    picked = jnp.dot(hot[...], stacked[...], preferred_element_type=jnp.float32)
    frame = (*outs[0].shape[:1], 2, *outs[0].shape[2:])
    picked = picked.astype(jnp.bfloat16).reshape(frame)
    kinds = outs[0].shape[1]
    for part, out in enumerate(outs):
        out[...] = picked[:, part * kinds : (part + 1) * kinds]


def fixed(shape):
    return pl.BlockSpec(shape, lambda i: (0,) * len(shape))


def pick(code_rows, place_columns, rows_pair, norm=None, part=0):
    length, width = rows_pair[1].shape
    all_slots = place_columns[0].shape[0]
    step = block_width(width)
    outs = 1
    skip = part * (width // step)
    frame = (all_slots // (4 * CAP), 2 // outs, 2 * CAP)
    block = pl.BlockSpec((length, step), lambda i: (0, i))
    extra, extra_specs = (), []
    if norm is not None:
        gain, near_inv, far_inv = norm
        extra = (gain, near_inv, far_inv)
        extra_specs = [pl.BlockSpec((1, step), lambda i: (0, i))] + [fixed((length, 1))] * 2
    return pl.pallas_call(
        functools.partial(pick_kernel, norm is not None),
        out_shape=[jax.ShapeDtypeStruct((*frame, width), jnp.bfloat16)] * outs,
        grid=(width // step,),
        in_specs=[fixed((TOP, length))] * 2
        + [fixed((all_slots, 1))] * 2
        + extra_specs
        + [pl.BlockSpec((length, step), lambda i: (0, i + skip)), block],
        out_specs=[pl.BlockSpec((*frame, step), lambda i: (0, 0, 0, i))] * outs,
        scratch_shapes=[
            pltpu.VMEM((all_slots, 2 * length), jnp.bfloat16),
            pltpu.VMEM((2 * length, step), jnp.bfloat16),
        ],
        compiler_params=pltpu.CompilerParams(vmem_limit_bytes=60 << 20),
        cost_estimate=pl.CostEstimate(
            flops=4 * all_slots * length * width,
            bytes_accessed=2 * width * (2 * length + all_slots),
            transcendentals=0,
        ),
        name="pn" if norm is not None else "pg",
    )(*code_rows, *place_columns, *extra, *rows_pair)


def gate_matrix(codes, place, gates, high, low):
    length = codes[0].shape[0]
    for side in (0, 1):
        exact = jnp.zeros((length, high.shape[1]), jnp.float32)
        for k in range(TOP):
            exact = jnp.where(
                codes[side][:, k : k + 1] == place[side][...], gates[side][:, k : k + 1], exact
            )
        rows = slice(side * length, (side + 1) * length)
        high_part = exact.astype(jnp.bfloat16)
        high[rows, :] = high_part
        low[rows, :] = (exact - high_part.astype(jnp.float32)).astype(jnp.bfloat16)


def weighted(high, low, rows):
    return jnp.dot(high[...], rows, preferred_element_type=jnp.float32) + jnp.dot(
        low[...], rows, preferred_element_type=jnp.float32
    )


def forward_kernel(*refs):
    codes, place, gates = refs[0:2], refs[2:4], refs[4:6]
    back, near_g, far_g, state, near_out, far_out, sums_out, high, low, overlap = refs[6:]
    length, step = near_out.shape
    index = pl.program_id(0)

    @pl.when(index == 0)
    def _():
        gate_matrix(codes, place, gates, high, low)
        overlap[...] = jnp.zeros_like(overlap)

    rows = back[...].reshape(-1, step)
    mixed = weighted(high, low, rows)
    near_out[...] = mixed[:length] + state[...].astype(jnp.float32)
    far_out[:, pl.ds(pl.multiple_of(index * step, step), step)] = mixed[length:].astype(
        jnp.bfloat16
    )
    for side, grads in enumerate((near_g, far_g)):
        overlap[side * length : (side + 1) * length, :] += lax.dot_general(
            grads[...], rows, (((1,), (1,)), ((), ())), preferred_element_type=jnp.float32
        )

    @pl.when(index == pl.num_programs(0) - 1)
    def _():
        sums = [
            [
                jnp.sum(
                    jnp.where(
                        codes[side][:, k : k + 1] == place[side][...],
                        overlap[side * length : (side + 1) * length, :],
                        0.0,
                    ),
                    axis=1,
                    keepdims=True,
                )
                for k in range(TOP)
            ]
            for side in (0, 1)
        ]
        lane = lax.broadcasted_iota(jnp.int32, sums_out.shape, 1)
        spread = jnp.zeros(sums_out.shape, jnp.float32)
        for k in range(TOP):
            spread = jnp.where(lane == k, sums[0][k], spread)
        sums_out[...] = spread
        far_out[:, far_out.shape[1] - HEAD_DIM :] = packed_tail(sums[1])


def combine_specs(length, all_slots):
    return (
        [fixed((length, TOP))] * 2 + [fixed((1, all_slots))] * 2 + [fixed((length, TOP))] * 2
    )


def combine_forward(codes, place, gates, back, grad_pair, state):
    length, width = state.shape
    all_slots = place[0].shape[1]
    step = block_width(width)
    block = pl.BlockSpec((length, step), lambda i: (0, i))
    slot_block = pl.BlockSpec((*back.shape[:3], step), lambda i: (0, 0, 0, i))
    return pl.pallas_call(
        forward_kernel,
        out_shape=[
            jax.ShapeDtypeStruct((length, width), jnp.float32),
            jax.ShapeDtypeStruct((length, width + HEAD_DIM), jnp.bfloat16),
            jax.ShapeDtypeStruct((length, HEAD_DIM), jnp.float32),
        ],
        grid=(width // step,),
        in_specs=combine_specs(length, all_slots) + [slot_block] + [block] * 3,
        out_specs=[block, fixed((length, width + HEAD_DIM)), fixed((length, HEAD_DIM))],
        scratch_shapes=[pltpu.VMEM((2 * length, all_slots), jnp.bfloat16)] * 2
        + [pltpu.VMEM((2 * length, all_slots), jnp.float32)],
        compiler_params=pltpu.CompilerParams(vmem_limit_bytes=60 << 20),
        cost_estimate=pl.CostEstimate(
            flops=12 * length * all_slots * width,
            bytes_accessed=2 * all_slots * width + 12 * length * width,
            transcendentals=0,
        ),
        name="cf",
    )(*codes, *place, *gates, back, *grad_pair, state)


def backward_kernel(*refs):
    codes, place, gates = refs[0:2], refs[2:4], refs[4:6]
    back, near_state, far_state, gain = refs[6:10]
    near_out, far_out, dot_out, high, low, dots = refs[10:]
    length, step = near_out.shape
    index = pl.program_id(0)

    @pl.when(index == 0)
    def _():
        gate_matrix(codes, place, gates, high, low)
        dots[...] = jnp.zeros_like(dots)

    mixed = weighted(high, low, back[...].reshape(-1, step))
    near, far = mixed[:length], mixed[length:]
    near_out[...] = near
    far_out[...] = far.astype(jnp.bfloat16)
    for side, (grads, state) in enumerate(((near, near_state), (far, far_state))):
        dots[side] += jnp.sum(
            grads * (state[...].astype(jnp.float32) * gain[...]), axis=1, keepdims=True
        )

    @pl.when(index == pl.num_programs(0) - 1)
    def _():
        dot_out[...] = dots[...]


def combine_backward(part, codes, place, gates, back, state_pair, gain):
    length = state_pair[0].shape[0]
    width = back.shape[3]
    all_slots = place[0].shape[1]
    step = block_width(width)
    skip = part * (width // step)
    block = pl.BlockSpec((length, step), lambda i: (0, i))
    shifted = pl.BlockSpec((length, step), lambda i: (0, i + skip))
    slot_block = pl.BlockSpec((*back.shape[:3], step), lambda i: (0, 0, 0, i))
    return pl.pallas_call(
        backward_kernel,
        out_shape=[
            jax.ShapeDtypeStruct((length, width), jnp.float32),
            jax.ShapeDtypeStruct((length, width), jnp.bfloat16),
            jax.ShapeDtypeStruct((2, length, 1), jnp.float32),
        ],
        grid=(width // step,),
        in_specs=combine_specs(length, all_slots)
        + [slot_block]
        + [shifted] * 2
        + [pl.BlockSpec((1, step), lambda i: (0, i + skip))],
        out_specs=[block, block, fixed((2, length, 1))],
        scratch_shapes=[pltpu.VMEM((2 * length, all_slots), jnp.bfloat16)] * 2
        + [pltpu.VMEM((2, length, 1), jnp.float32)],
        compiler_params=pltpu.CompilerParams(vmem_limit_bytes=60 << 20),
        cost_estimate=pl.CostEstimate(
            flops=8 * length * all_slots * width,
            bytes_accessed=2 * all_slots * width + 10 * length * width,
            transcendentals=0,
        ),
    )(*codes, *place, *gates, back, *state_pair, gain)


STREAMS = 4


def narrow_kernel(rows_last, amount, *refs):
    xs = refs[:amount]
    *weights, out, total = refs[amount:]
    index = pl.program_id(1)
    each = pl.num_programs(1) // amount

    @pl.when(index == 0)
    def _():
        total[...] = jnp.zeros_like(total)

    def add(x):
        rows = x[...].reshape(total.shape[0], x.shape[3])
        share = x.shape[3] // len(weights)
        total[...] += sum(
            lax.dot_general(
                rows[:, i * share : (i + 1) * share],
                weight[0, 0],
                (((1,), (1 if rows_last else 0,)), ((), ())),
                preferred_element_type=jnp.float32,
            )
            for i, weight in enumerate(weights)
        )

    for turn, x in enumerate(xs):
        pl.when(index // each == turn)(functools.partial(add, x))

    @pl.when(index == pl.num_programs(1) - 1)
    def _():
        out[0] = total[...].astype(jnp.bfloat16)


def to_hidden(xs, weight, rows_last):
    half, kinds, run, part_width = xs[0].shape
    width = part_width * len(xs)
    hidden = weight.shape[2 if rows_last else 3]
    step = min(1024, part_width)
    each = part_width // step
    share = step // STREAMS
    rows = half * run
    if rows_last:
        weight_specs = [
            pl.BlockSpec((1, 1, hidden, share), lambda k, j, i=i: (k, 0, 0, j * STREAMS + i))
            for i in range(STREAMS)
        ]
    else:
        weight_specs = [
            pl.BlockSpec((1, 1, share, hidden), lambda k, j, i=i: (k, 0, j * STREAMS + i, 0))
            for i in range(STREAMS)
        ]
    return pl.pallas_call(
        functools.partial(narrow_kernel, rows_last, len(xs)),
        out_shape=jax.ShapeDtypeStruct((kinds, rows, hidden), jnp.bfloat16),
        grid=(kinds, width // step),
        in_specs=[
            pl.BlockSpec(
                (half, 1, run, step),
                lambda k, j, i=i: (0, k, 0, jnp.clip(j - i * each, 0, each - 1)),
            )
            for i in range(len(xs))
        ]
        + weight_specs,
        out_specs=pl.BlockSpec((1, rows, hidden), lambda k, j: (k, 0, 0)),
        scratch_shapes=[pltpu.VMEM((rows, hidden), jnp.float32)],
        compiler_params=pltpu.CompilerParams(vmem_limit_bytes=60 << 20),
        cost_estimate=pl.CostEstimate(
            flops=2 * kinds * rows * width * hidden,
            bytes_accessed=2 * kinds * width * (hidden + rows),
            transcendentals=0,
        ),
    )(*xs, *[weight] * STREAMS)


def widen_kernel(rows_last, hidden, *refs):
    *weights, out = refs
    share = out.shape[3] // len(weights)
    for i, weight in enumerate(weights):
        wide = lax.dot_general(
            hidden[0],
            weight[0, 0],
            (((1,), (1 if rows_last else 0,)), ((), ())),
            preferred_element_type=jnp.float32,
        )
        out[:, :, :, i * share : (i + 1) * share] = wide.astype(jnp.bfloat16).reshape(
            *out.shape[:3], share
        )


def from_hidden(hidden, weight, rows_last, half, part=0, parts=1):
    kinds, rows, inner = hidden.shape
    width = weight.shape[2 if rows_last else 3] // parts
    run = rows // half
    step = min(1024, width)
    share = step // STREAMS
    skip = part * (width // share)
    if rows_last:
        weight_specs = [
            pl.BlockSpec((1, 1, share, inner), lambda k, j, i=i: (k, 0, j * STREAMS + i + skip, 0))
            for i in range(STREAMS)
        ]
    else:
        weight_specs = [
            pl.BlockSpec((1, 1, inner, share), lambda k, j, i=i: (k, 0, 0, j * STREAMS + i + skip))
            for i in range(STREAMS)
        ]
    return pl.pallas_call(
        functools.partial(widen_kernel, rows_last),
        out_shape=jax.ShapeDtypeStruct((half, kinds, run, width), jnp.bfloat16),
        grid=(kinds, width // step),
        in_specs=[pl.BlockSpec((1, rows, inner), lambda k, j: (k, 0, 0)), *weight_specs],
        out_specs=pl.BlockSpec((half, 1, run, step), lambda k, j: (0, k, 0, j)),
        compiler_params=pltpu.CompilerParams(vmem_limit_bytes=60 << 20),
        cost_estimate=pl.CostEstimate(
            flops=2 * kinds * rows * width * inner,
            bytes_accessed=2 * kinds * width * (inner + rows),
            transcendentals=0,
        ),
    )(hidden, *[weight] * STREAMS)


def body(
    inputs,
    query_states,
    key_states,
    value_states,
    doc_ids,
    modality,
    expert_ids,
    norm_gain,
    router_w,
    w_in,
    w_out,
    grad_out,
):
    length, width_local = inputs.shape
    experts = lax.axis_size("seq")
    half = experts // 2
    slots = experts * CAP

    kept_mask = expert_ids >= 0
    kept_wide = kept_mask.astype(jnp.float32)
    column = modality[:, None] * experts + jnp.where(kept_mask, expert_ids, 0)
    one_hot = (
        column[:, :, None] == jnp.arange(2 * experts, dtype=jnp.int32)[None, None, :]
    ) & kept_mask[:, :, None]
    entries = length * TOP
    flat_hot = one_hot.reshape(entries, 2 * experts).astype(jnp.bfloat16)
    entry_range = jnp.arange(entries, dtype=jnp.int32)
    earlier = (entry_range[:, None] > entry_range[None, :]).astype(jnp.bfloat16)
    before = jnp.dot(earlier, flat_hot, preferred_element_type=jnp.float32)
    slot_rank = jnp.sum(before * flat_hot.astype(jnp.float32), axis=1).astype(jnp.int32)
    slot_index = jnp.where(kept_mask, column * CAP + slot_rank.reshape(length, TOP), -1)

    position = jnp.arange(2 * slots, dtype=jnp.int32)
    first = lax.axis_index("seq") // half * half * CAP
    kind_of = position // (2 * CAP) % 2
    place = kind_of * slots + first + position // (4 * CAP) * CAP + position % CAP
    side_of = position // CAP % 2
    places = [jnp.where(side_of == side, place, -2) for side in (0, 1)]
    place_rows = [one.reshape(1, 2 * slots) for one in places]
    place_columns = [one.reshape(2 * slots, 1) for one in places]

    pieces, far_index, grad_far = gather_pieces(key_states, value_states, slot_index, grad_out)
    codes = [slot_index, far_index]
    code_rows = [one.T for one in codes]
    grad_fars = [grad_far, far_swap(grad_out[:, width_local // 2 :])]
    grad_pair = [grad_out, jnp.concatenate(grad_fars, axis=1)]

    attended = attend(query_states, pieces, doc_ids)
    resid_state = (inputs.astype(jnp.float32) + attended.astype(jnp.float32)).astype(jnp.bfloat16)
    state_pair = [resid_state, far_swap(resid_state)]
    state_wide = resid_state.astype(jnp.float32)
    gain = norm_gain[None, :]
    squares = row_total(jnp.sum(state_wide * state_wide, axis=1))
    inv_rms = lax.rsqrt(squares / D + eps_norm)[:, None]
    normed = (state_wide * gain * inv_rms).astype(jnp.bfloat16)
    logits = row_total(jnp.dot(normed, router_w, preferred_element_type=jnp.float32))
    chosen = jnp.sum(jnp.where(one_hot, logits[:, None, :], 0.0), axis=2)
    lifted = jax.nn.sigmoid(chosen)
    denominator = gate_offset + jnp.sum(kept_wide * lifted, axis=1, keepdims=True)
    gates = kept_wide * lifted / denominator
    far_scalars = far_swap(jnp.concatenate([gates, inv_rms], axis=1))
    gate_pair = [gates, far_scalars[:, :TOP]]
    far_inv = far_scalars[:, TOP:]

    got_rows = half_exchange(
        pick(code_rows, place_columns, state_pair, (gain, inv_rms, far_inv))[0]
    )

    got_grads = [
        half_exchange(pick(code_rows, place_columns, (grad_out, far), part=part)[0])
        for part, far in enumerate(grad_fars)
    ]
    act_grad = whole_hidden(to_hidden(got_grads, w_out, True))
    pre_act = whole_hidden(to_hidden([got_rows], w_in, False))
    active = jax.nn.gelu(pre_act, approximate=True).astype(jnp.bfloat16)
    expert_out = from_hidden(active, w_out, False, half)
    returned = half_exchange(expert_out)
    pre_later, _ = lax.optimization_barrier((pre_act, expert_out))
    pre_grad = gelu_back(pre_later, act_grad).astype(jnp.bfloat16)
    near_sum, far_sum, near_overlap = combine_forward(
        codes, place_rows, gate_pair, returned, grad_pair, resid_state
    )
    got_sum = far_swap(far_sum)
    layer_out = (near_sum + got_sum[:, :width_local].astype(jnp.float32)).astype(jnp.bfloat16)

    gate_grad = row_total(near_overlap[:, :TOP] + unpack_tail(got_sum[:, width_local:], TOP))
    gate_dot = jnp.sum(gates * gate_grad, axis=1, keepdims=True)
    logit_grad = kept_wide * (gate_grad - gate_dot) / denominator * lifted * (1.0 - lifted)
    logit_full = jnp.sum(jnp.where(one_hot, logit_grad[:, :, None], 0.0), axis=1)
    router_grad = jnp.dot(
        logit_full, router_w.astype(jnp.float32).T, precision=lax.Precision.HIGHEST
    )
    parts = 2
    near_grads, far_grads, dots = [], [], []
    for part in range(parts):
        entry_grad = from_hidden(pre_grad, w_in, True, half, part, parts)
        near, far, dot = combine_backward(
            part, codes, place_rows, gate_pair, half_exchange(entry_grad), state_pair, gain
        )
        far = far_swap(far)
        near_grads.append(near)
        far_grads.append(far)
        dots.append(dot)
    dots = sum(dots)
    far_dot = far_swap(dots[1])
    near_grad = jnp.concatenate(near_grads, axis=1)
    got_grad = jnp.concatenate(far_grads, axis=1)
    router_dot = jnp.sum(router_grad * (state_wide * gain), axis=1, keepdims=True)
    norm_dot = row_total(dots[0] + far_dot + router_dot)
    state_grad = (
        grad_out.astype(jnp.float32)
        + inv_rms * gain * (router_grad + near_grad + got_grad.astype(jnp.float32))
        - inv_rms**3 / D * state_wide * norm_dot
    )
    return (layer_out, state_grad.astype(jnp.bfloat16))


def solution(mesh):
    in_specs = (
        P("seq", "grp"),
        P("seq", "grp"),
        P("seq", "grp"),
        P("seq", "grp"),
        P(),
        P("seq"),
        P("seq", None),
        P("grp"),
        P("grp", None),
        P(None, "seq", "grp", None),
        P(None, "seq", None, "grp"),
        P("seq", "grp"),
    )
    out_specs = (P("seq", "grp"), P("seq", "grp"))

    return jax.shard_map(body, mesh=mesh, in_specs=in_specs, out_specs=out_specs, check_vma=False)
```
